32 devices in a mesh: dp: 8 (over z, y), expert: 4 (over x, core).
Axes of the slice: x: 2, y: 2, z: 4, core: 2. Of those that a mesh axis runs over, the one named last changes fastest.
Arguments:
- tokens: bfloat16 [1024, 4096], P('dp'), may hold values from -6 to 6
- upstream: bfloat16 [1024, 4096], P('dp', 'expert'), may hold values from -6 to 6
- gates: bfloat16 [1024, 2], P('dp'), may hold values from 0.049804688 to 1
- expert_ids: int32 [1024, 2], P('dp'), may hold values from 0 to 7, all different within a row; in each aligned block of 128 rows (0 to 127, 128 to 255, ...) at most 64 rows name the same one
- w_gate: bfloat16 [8, 1536, 4096], P('dp', 'expert'), may hold values from -0.09375 to 0.09375
- w_up: bfloat16 [8, 1536, 4096], P('dp', 'expert'), may hold values from -0.09375 to 0.09375
- w_down: bfloat16 [8, 1536, 4096], P('dp', 'expert'), may hold values from -0.15625 to 0.15625
Outputs:
- grad_x: bfloat16 [1024, 4096], P('dp', 'expert')
- grad_gates: float32 [1024, 2], P('dp')
- grad_w_gate: bfloat16 [8, 1536, 4096], P('dp', 'expert')
- grad_w_up: bfloat16 [8, 1536, 4096], P('dp', 'expert')
- grad_w_down: bfloat16 [8, 1536, 4096], P('dp', 'expert')
The draws below stay inside these ranges and needn't reach their ends.
Inputs may be any that keep to these rules, and one draw needn't show every extreme that they name: `expert_ids`: each row names 2 different experts. In each aligned block of 128 rows (the tokens of one index of dp) no expert is named by more than 64 rows, a bound that some block reaches.
All inputs are finite; a program needn't handle non-finite values.
Results may differ from the reference program's by a relative error of at most 0.012.
Values may be sent and summed in bfloat16 or wider, within the bound.
A program may use at most 128 MiB of HBM per device.

```python
import math
import jax
import jax.numpy as jnp
import numpy as np
from jax import lax

D = 4096
HID = 1536
TOK_DEV = 128
TOP = 2
EXPERTS = 8
CAP = 64
TOKENS = 1024
N_DP = 8
N_EXPERT = 4


def shard_levels(stream_key, extent, pieces, low, top_value):
    def one(dim, blocks):
        steps = jax.random.uniform(jax.random.fold_in(jax.random.fold_in(stream_key, 6), dim), (blocks,), jnp.float32, low / len(pieces), top_value / len(pieces))
        return jnp.repeat(jnp.exp(steps), extent[dim] // blocks).reshape((-1,) + (1,) * (len(extent) - dim - 1))

    level = one(*pieces[0])
    for cut in pieces[1:]:
        level = level * one(*cut)
    return level


def shared_out(key, own, number, rows, number_of, top, bound, lean):
    ranking = jax.random.permutation(key, number_of)
    crowded, usual = shares(number_of, rows * top, bound, lean, True), shares(number_of, rows * top, bound, lean, False)
    places = jnp.arange(number_of)

    def named(lengths, turn):
        used = int((lengths > 0).sum())
        fixed = max(1, used // 4)
        moved = fixed + (places - fixed + turn * (used - fixed)) % max(1, number_of - fixed)
        return jnp.zeros((number_of,), jnp.int32).at[ranking[jnp.where(places < fixed, places, moved)]].set(jnp.asarray(lengths, jnp.int32))

    lengths = jnp.where(number % 4 == 0, named(crowded, number // 4), named(usual, number - number // 4 - 1))
    mixed = jax.random.permutation(jax.random.fold_in(own, 3), number_of)
    donor, taker = mixed[0:number_of // 2 * 2:2], mixed[1:number_of // 2 * 2:2]
    margin = jnp.minimum(lengths[donor] - 1, bound - lengths[taker]) // 2
    margin = jnp.where((donor == ranking[0]) | (taker == ranking[0]) | (lengths[taker] == 0), 0, jnp.maximum(margin, 0))
    moved = jax.random.randint(jax.random.fold_in(own, 4), (number_of // 2,), 0, 1 << 20) % (margin + 1)
    lengths = lengths.at[donor].add(-moved).at[taker].add(moved)
    members = jnp.searchsorted(jnp.cumsum(lengths), jnp.arange(rows * top), side="right").astype(jnp.int32)
    table = members.reshape(top, rows).T
    table = table[jax.random.permutation(jax.random.fold_in(own, 1), rows)]
    turn = jax.random.randint(jax.random.fold_in(own, 2), (rows, 1), 0, top)
    return jnp.take_along_axis(table, (jnp.arange(top)[None, :] + turn) % top, axis=1)


def shares(number_of, total, most, skew, full):
    weights = [(1 << 20) // math.isqrt(rank ** skew) + 1 for rank in range(1, number_of + 1)]
    largest = most if full else min(most, max(-(-total // number_of), total * weights[0] // sum(weights)))
    least = 1 if total - largest >= number_of - 1 else 0
    holding, rest = [largest] + [least] * (number_of - 1), total - largest - least * (number_of - 1)
    while rest > 0:
        free = [i for i in range(1, number_of) if holding[i] < largest] or [i for i in range(1, number_of) if holding[i] < most]
        mass, left = sum([weights[i] for i in free]), rest
        for i in free:
            more = min(most - holding[i], max(1, left * weights[i] // mass), rest)
            holding[i] = holding[i] + more
            rest = rest - more
    return np.array(holding)


def noise(stream_key, dims, scale, reach, split=(), kind=jnp.bfloat16):
    values = scale * jax.random.normal(stream_key, dims, jnp.float32)
    if split:
        values = values * shard_levels(stream_key, dims, split, -0.22, 0.18)
    return jnp.clip(values, -reach, reach).astype(kind)


def setup_inputs(seed: int = 0) -> dict:
    splits = jax.random.split(jax.random.key(seed), 8)
    tokens = noise(splits[0], (TOKENS, D), 1.0, 6.0, ((0, 8),))
    upstream = noise(splits[1], (TOKENS, D), 1.0, 6.0, ((0, 8), (1, 4)))
    gates = jnp.clip(jnp.exp(math.log(1.0) - 2.9996462 * jax.random.uniform(splits[2], (TOKENS, TOP), jnp.float32) ** shard_levels(splits[2], (TOKENS, TOP), ((0, 8),), -0.2, 0.2)), 0.049804688, 1.0).astype(jnp.bfloat16)
    expert_ids_keys = jax.random.split(jax.random.fold_in(splits[3], 1), TOKENS // TOK_DEV)
    expert_ids_turns = jax.random.permutation(jax.random.fold_in(splits[3], 3), TOKENS // TOK_DEV)
    expert_ids = jax.vmap(lambda own, number: shared_out(jax.random.fold_in(splits[3], 2), own, number, TOK_DEV, EXPERTS, TOP, CAP, 2))(expert_ids_keys, expert_ids_turns).reshape((TOKENS, TOP))
    w_gate = noise(splits[4], (EXPERTS, HID, D), D ** -0.5, 0.09375, ((0, 8), (1, 4)))
    w_up = noise(splits[5], (EXPERTS, HID, D), D ** -0.5, 0.09375, ((0, 8), (1, 4)))
    w_down = noise(splits[6], (EXPERTS, HID, D), HID ** -0.5, 0.15625, ((0, 8), (1, 4)))
    return dict(tokens=tokens, upstream=upstream, gates=gates, expert_ids=expert_ids, w_gate=w_gate, w_up=w_up, w_down=w_down)


def swish_pair(pre):
    sigma = jax.nn.sigmoid(pre)
    return pre * sigma, sigma * (1.0 + pre * (1.0 - sigma))


def contract_last(left, right):
    return lax.dot_general(left, right, (((1,), (1,)), ((), ())), preferred_element_type=jnp.float32)


def contract_first(left, right):
    return lax.dot_general(left, right, (((0,), (0,)), ((), ())), preferred_element_type=jnp.float32)


def reference(tokens, upstream, gates, expert_ids, w_gate, w_up, w_down):
    experts = w_gate.shape[0]
    hidden = w_gate.shape[1]
    width = tokens.shape[1]
    top = expert_ids.shape[1]
    groups = N_DP
    windows = N_EXPERT
    window = hidden // windows
    tok_rows = tokens.shape[0] // groups
    cap = 2 * tok_rows * top // experts
    rows = groups * cap
    block_ids = expert_ids.reshape(groups, tok_rows * top)
    onehot = (block_ids[:, :, None] == jnp.arange(experts, dtype=jnp.int32)[None, None, :]).astype(jnp.int32)
    position = jnp.sum((jnp.cumsum(onehot, axis=1) - onehot) * onehot, axis=2).astype(jnp.int32)
    blocks = jnp.arange(groups, dtype=jnp.int32)[:, None]
    slot = ((block_ids * groups + blocks) * cap + position).reshape(-1).astype(jnp.int32)
    count = slot.shape[0]
    owner = jnp.zeros((experts * rows,), jnp.int32).at[slot].set(jnp.arange(count, dtype=jnp.int32) + 1)
    owner = owner.reshape(experts, rows)
    flat_gates = gates.reshape(-1)

    def per_expert(packed):
        own, w_g, w_u, w_d = packed
        live = own > 0
        source = jnp.maximum(own - 1, 0)
        token_of = source // top
        inputs = jnp.where(live[:, None], tokens[token_of], jnp.zeros((), tokens.dtype))
        upward = jnp.where(live[:, None], upstream[token_of], jnp.zeros((), upstream.dtype))
        scales = jnp.where(live, flat_gates[source], jnp.zeros((), gates.dtype))
        pre_gate = contract_last(inputs, w_g)
        pre_up = contract_last(inputs, w_u)
        swish, slope = swish_pair(pre_gate)
        act = (swish * pre_up).astype(jnp.bfloat16)
        act_f = act.astype(jnp.float32)
        back = contract_last(upward, w_d)
        gate_term = jnp.sum(act_f * back, axis=1)
        scale_col = scales.astype(jnp.float32)[:, None]
        scaled = (scale_col * act_f).astype(jnp.bfloat16)
        grad_down = contract_first(scaled, upward).astype(jnp.bfloat16)
        weighted = scale_col * back
        d_gate = (weighted * pre_up * slope).astype(jnp.bfloat16)
        d_up = (weighted * swish).astype(jnp.bfloat16)
        grad_gate = contract_first(d_gate, inputs).astype(jnp.bfloat16)
        grad_up = contract_first(d_up, inputs).astype(jnp.bfloat16)
        total = jnp.zeros((rows, width), jnp.float32)
        for index in range(windows):
            low = index * window
            high = low + window
            piece = jnp.dot(d_gate[:, low:high], w_g[low:high], preferred_element_type=jnp.float32)
            piece = piece + jnp.dot(d_up[:, low:high], w_u[low:high], preferred_element_type=jnp.float32)
            piece = lax.optimization_barrier(piece.astype(jnp.bfloat16))
            total = total + piece.astype(jnp.float32)
        return total, gate_term, grad_gate, grad_up, grad_down

    totals, gate_terms, grad_w_gate, grad_w_up, grad_w_down = lax.map(per_expert, (owner, w_gate, w_up, w_down))
    totals = totals.reshape(experts * rows, width)
    gate_terms = gate_terms.reshape(-1)
    grad_x = jnp.sum(totals[slot].reshape(tokens.shape[0], top, width), axis=1).astype(jnp.bfloat16)
    grad_gates = gate_terms[slot].reshape(tokens.shape[0], top)
    return grad_x, grad_gates, grad_w_gate, grad_w_up, grad_w_down
```

```python
import functools

import jax
import jax.numpy as jnp
from jax import lax
from jax.experimental import pallas as pl
from jax.experimental.pallas import tpu as pltpu
from jax.sharding import PartitionSpec as P

MESH = pltpu.DeviceIdType.MESH if hasattr(pltpu, "DeviceIdType") else pl.DeviceIdType.MESH
LANES = 128


def contract_last(left, right):
    return lax.dot_general(
        left, right, (((1,), (1,)), ((), ())), preferred_element_type=jnp.float32
    )


def contract_first(left, right):
    return lax.dot_general(
        left, right, (((0,), (0,)), ((), ())), preferred_element_type=jnp.float32
    )


def matmul(left, right):
    return jnp.dot(left, right, preferred_element_type=jnp.float32)


def kernel(
    groups, parts,
    ids_ref, gates_ref, tok_hbm, ups_hbm, w_g_hbm, w_u_hbm, w_d_hbm,
    gx_out, gg_out, out_g, out_u, out_d,
    tok, ups, pick, send_t, send_u, recv_t, recv_u, weights, pre, flipped, straight,
    scale_send, scale_recv, scale_row, term, term_recv, total, home_s,
    pair_send, pair_recv, side_send, side_recv, own_sum, out_send, home, gx_acc,
    load_sem, w_sem, recv_sem, scale_sem, dp_near, dp_far, dp_up, pair_fwd, side_fwd,
    scale_out, pair_send_sem, pair_recv_sem, side_send_sem, side_recv_sem,
    home_send, home_recv, term_send, term_sem, back_send, back_recv,
):
    me, own = lax.axis_index("dp"), lax.axis_index("expert")
    core, place = lax.rem(own, 2), lax.div(own, 2)
    places = parts // 2
    partner = place * 2 + (1 - core)
    cap, part = send_u.shape[1:]
    top, count = ids_ref.shape
    rows = groups * cap
    hid = weights.shape[2]
    near = groups // 2
    per_tile = LANES // cap
    recvs = (recv_t, recv_u)
    quarter = (groups - near) // 2
    chunks = [(0, near), (near, quarter), (near + quarter, groups - near - quarter)]
    bf, f32 = jnp.bfloat16, jnp.float32

    def ahead(k):
        spot = me
        for bit in [1 << b for b in range(groups.bit_length()) if k >> b & 1]:
            spot = spot + bit * (1 - 2 * lax.rem(lax.div(me, bit), 2))
        return spot

    def aside(j):
        return lax.rem(place + j, places) * 2 + core

    def columns(r):
        j, other = divmod(r, 2)
        spot = lax.rem(place + j, places) * 2 + (1 - core if other else core)
        return pl.ds(pl.multiple_of(spot * part, part), part)

    def remote(src, dst, send_sem, sem, target):
        return pltpu.make_async_remote_copy(
            src_ref=src, dst_ref=dst, send_sem=send_sem, recv_sem=sem,
            device_id=target, device_id_type=MESH,
        )

    def arrived(ref, sem):
        pltpu.make_async_copy(ref, ref, sem).wait()

    barrier = pltpu.get_barrier_semaphore()
    for k in range(1, groups):
        pl.semaphore_signal(barrier, inc=1, device_id={"dp": ahead(k)}, device_id_type=MESH)
    for j in range(1, parts):
        pl.semaphore_signal(
            barrier, inc=1, device_id={"expert": lax.rem(own + j, parts)}, device_id_type=MESH
        )

    feeds = [
        pltpu.make_async_copy(tok_hbm.at[:, columns(2 * j)], tok.at[j], load_sem.at[j])
        for j in range(places)
    ]
    feeds.append(pltpu.make_async_copy(ups_hbm, ups, load_sem.at[places]))
    for feed in feeds:
        feed.start()
    step_of = lax.broadcasted_iota(jnp.int32, (groups, count), 0)
    expert = jnp.zeros((groups, count), jnp.int32)
    for k in range(groups):
        expert = jnp.where(step_of == k, ahead(k), expert)
    named = [ids_ref[j : j + 1, :] == expert for j in range(top)]
    member = jnp.zeros((groups, count), f32)
    weight = jnp.zeros((groups, count), f32)
    gates = gates_ref[...].astype(f32)
    for j in range(top):
        member = jnp.where(named[j], 1.0, member)
        weight = jnp.where(named[j], gates[j : j + 1, :], weight)
    earlier = (
        lax.broadcasted_iota(jnp.int32, (count, count), 0)
        < lax.broadcasted_iota(jnp.int32, (count, count), 1)
    )
    before = matmul(member.astype(bf), jnp.where(earlier, 1.0, 0.0).astype(bf))
    place_of = jnp.where(member > 0.5, before, -1.0)
    slot_of = lax.broadcasted_iota(jnp.int32, (cap, count), 0).astype(f32)
    for k in range(groups):
        hit = place_of[k : k + 1, :] == slot_of
        pick[pl.ds(k * cap, cap), :] = jnp.where(hit, 1.0, 0.0).astype(bf)

    lane = lax.broadcasted_iota(jnp.int32, (groups, rows), 1)
    first = lax.broadcasted_iota(jnp.int32, (groups, rows), 0) * cap
    own_block = (lane >= first) & (lane < first + cap)
    scales = contract_last(weight.astype(bf), pick[...])
    scales = jnp.sum(jnp.where(own_block, scales, 0.0), axis=0, keepdims=True)
    for i in range(rows // LANES):
        scale_send[i] = jnp.broadcast_to(scales[:, i * LANES : (i + 1) * LANES], (8, LANES))

    block_steps = per_tile

    def gather(b):
        at = pl.ds(b * LANES, LANES)
        steps = range(b * block_steps, (b + 1) * block_steps)
        for j in range(places if steps[0] < near else 1):
            value = matmul(pick[at, :], tok[j]).astype(bf).reshape(block_steps, cap, part)
            for i, k in enumerate(steps):
                if k:
                    send_t[j, k] = value[i]
                else:
                    recv_t[2 * j, 0] = value[i]
        value = matmul(pick[at, :], ups[...]).astype(bf).reshape(block_steps, cap, part)
        for i, k in enumerate(steps):
            if k:
                send_u[k] = value[i]
            else:
                recv_u[0, 0] = value[i]

    def dispatch(b):
        for k in range(b * block_steps, (b + 1) * block_steps):
            if k == 0:
                continue
            to = {"dp": ahead(k)}
            remote(scale_send.at[k // per_tile], scale_recv.at[k], scale_out, scale_sem.at[k],
                   to).start()
            if k < near:
                for j in range(places):
                    remote(send_t.at[j, k], recv_t.at[2 * j, k], dp_near,
                           recv_sem.at[0, 2 * j, k], to).start()
            else:
                remote(send_t.at[0, k], recv_t.at[0, k], dp_far, recv_sem.at[0, 0, k], to).start()
            remote(send_u.at[k], recv_u.at[0, k], dp_up, recv_sem.at[1, 0, k], to).start()

    with jax.named_scope("feedwait"):
        for feed in feeds:
            feed.wait()
    blocks = rows // LANES
    near_blocks = near // block_steps
    order = list(range(1, near_blocks)) + [0] + list(range(near_blocks, blocks))
    with jax.named_scope("gather0"):
        gather(order[0])
    with jax.named_scope("A_barrier"):
        pl.semaphore_wait(barrier, groups + parts - 2)
    dispatch(order[0])
    for b in order[1:]:
        gather(b)
        dispatch(b)

    loads = []
    for m, w_hbm in enumerate((w_g_hbm, w_u_hbm, w_d_hbm)):
        for r in range(parts):
            load = pltpu.make_async_copy(w_hbm.at[:, columns(r)], weights.at[m, r], w_sem.at[m, r])
            load.start()
            loads.append(load)

    def relay(t, k):
        if t == 0 and k < near:
            for j in range(places):
                spot = recv_t.at[2 * j, k]
                if k:
                    arrived(spot, recv_sem.at[0, 2 * j, k])
                remote(spot, recv_t.at[2 * j + 1, k], pair_fwd.at[0],
                       recv_sem.at[0, 2 * j + 1, k], {"expert": partner}).start()
            return
        spot = recvs[t].at[0, k]
        if k:
            arrived(spot, recv_sem.at[t, 0, k])
        for j in range(1, places):
            r = 2 * (places - j)
            remote(spot, recvs[t].at[r, k], side_fwd.at[t], recv_sem.at[t, r, k],
                   {"expert": aside(j)}).start()
        remote(spot, recvs[t].at[1, k], pair_fwd.at[t], recv_sem.at[t, 1, k],
               {"expert": partner}).start()

    def pass_on(t, k):
        if t == 0 and k < near:
            return
        for j in range(1, places):
            spot = recvs[t].at[2 * j, k]
            arrived(spot, recv_sem.at[t, 2 * j, k])
            remote(spot, recvs[t].at[2 * j + 1, k], pair_fwd.at[t],
                   recv_sem.at[t, 2 * j + 1, k], {"expert": partner}).start()

    def finish(c):
        lo, n = chunks[c]
        for t in range(2):
            for k in range(lo, lo + n):
                for j in range(places):
                    arrived(recvs[t].at[2 * j + 1, k], recv_sem.at[t, 2 * j + 1, k])

    def forward_unit(c, m, r):
        lo, n = chunks[c]
        if c == 0:
            loads[m * parts + r].wait()
        at = pl.ds(lo * cap, n * cap)
        block = recvs[m // 2][r, pl.ds(lo, n)].reshape(n * cap, part)
        value = contract_last(weights[m, r], block)
        if r == 0:
            pre[m, :, at] = value
        else:
            pre[m, :, at] = pre[m, :, at] + value

    def mine(k, shape):
        spot = lax.broadcasted_iota(jnp.int32, shape, 1)
        low = k % per_tile * cap
        return (spot >= low) & (spot < low + cap)

    def merge_tile(i, source):
        value = jnp.zeros((8, LANES), f32)
        for k in range(i * per_tile, (i + 1) * per_tile):
            value = jnp.where(mine(k, (8, LANES)), source(k), value)
        return value

    tile = 32

    def elementwise(c):
        lo, n = chunks[c]
        at = pl.ds(lo * cap, n * cap)
        for k in range(max(lo, 1), lo + n):
            arrived(scale_recv.at[k], scale_sem.at[k])
        for i in range(lo // per_tile, (lo + n) // per_tile):
            scale_row[:, pl.ds(i * LANES, LANES)] = merge_tile(
                i, lambda k: scale_recv[k] if k else scale_send[0]
            )
        scale = scale_row[0:1, at]
        term[:, at] = jnp.zeros((8, n * cap), f32)

        @pl.loop(0, hid // tile)
        def _(step):
            spot = pl.ds(pl.multiple_of(step * tile, tile), tile)
            gate, up, back = pre[0, spot, at], pre[1, spot, at], pre[2, spot, at]
            sigma = jax.nn.sigmoid(gate)
            swish = gate * sigma
            slope = sigma * (1.0 + gate * (1.0 - sigma))
            act = (swish * up).astype(bf).astype(f32)
            term[:, at] += jnp.broadcast_to(
                jnp.sum(act * back, axis=0, keepdims=True), (8, n * cap)
            )
            weighted = scale * back
            flipped[0, spot, at] = (weighted * up * slope).astype(bf)
            flipped[1, spot, at] = (weighted * swish).astype(bf)
            flipped[2, spot, at] = (scale * act).astype(bf)

    def straighten(c):
        lo, n = chunks[c]
        at = pl.ds(lo * cap, n * cap)
        for m in range(2):
            straight[m, at, :] = jnp.transpose(flipped[m, :, at].astype(f32)).astype(bf)

    def piece(c, r):
        lo, n = chunks[c]
        at = pl.ds(lo * cap, n * cap)
        value = matmul(straight[0, at, :], weights[0, r])
        value = value + matmul(straight[1, at, :], weights[1, r])
        return value.reshape(n, cap, part)

    def pair(c, j):
        lo, n = chunks[c]
        at = pl.ds(lo, n)
        return remote(pair_send.at[j, at], pair_recv.at[j, at], pair_send_sem.at[j, c],
                      pair_recv_sem.at[j, c], {"expert": partner})

    def partial_other(c, j):
        lo, n = chunks[c]
        pair_send[j, pl.ds(lo, n)] = piece(c, 2 * j + 1).astype(bf)
        pair(c, j).start()

    def partial_own(c, j):
        lo, n = chunks[c]
        own_sum[j, pl.ds(lo, n)] = piece(c, 2 * j)

    def sideways(c, j, piece_of=0, pieces=1):
        lo, n = chunks[c]
        if piece_of == 0:
            pair(c, j).wait_recv()
        share = n // pieces
        for k in reversed(range(lo + n - (piece_of + 1) * share, lo + n - piece_of * share)):
            both = own_sum[j, k] + pair_recv[j, k].astype(f32)
            side_send[j, k] = both.astype(bf)
            remote(side_send.at[j, k], side_recv.at[j, k], side_send_sem.at[j],
                   side_recv_sem.at[j, k], {"expert": aside(j)}).start()

    def homeward(c, k):
        lo, n = chunks[c]
        if k == lo + n - 1:
            pair(c, 0).wait_recv()
        value = own_sum[0, k] + pair_recv[0, k].astype(f32)
        for j in range(1, places):
            arrived(side_recv.at[j, k], side_recv_sem.at[j, k])
            value = value + side_recv[j, k].astype(f32)
        if k == 0:
            home[0] = value.astype(bf)
        else:
            out_send[k] = value.astype(bf)
            remote(out_send.at[k], home.at[k], home_send, home_recv.at[k],
                   {"dp": ahead(k)}).start()

    def collect(c):
        lo, n = chunks[c]
        for k in range(max(lo, 1), lo + n):
            arrived(home.at[k], home_recv.at[k])
        value = contract_first(
            pick[pl.ds(lo * cap, n * cap), :], home[pl.ds(lo, n)].reshape(n * cap, part)
        )
        if c == 0:
            gx_acc[...] = value
        elif c < len(chunks) - 1:
            gx_acc[...] = gx_acc[...] + value
        else:
            gx_out[...] = (gx_acc[...] + value).astype(bf)

    def grad_unit(m, r):
        block = recvs[m // 2][r].reshape(rows, part)
        (out_g, out_u, out_d)[m][:, columns(r)] = matmul(flipped[m], block).astype(bf)

    def first_half(c):
        tasks = [functools.partial(forward_unit, c, m, r) for m in range(3) for r in range(parts)]
        tasks.append(functools.partial(elementwise, c))
        tasks.append(functools.partial(straighten, c))
        return tasks

    def second_half(c):
        tasks = []
        for j in list(range(1, places)) + [0]:
            tasks.append(functools.partial(partial_other, c, j))
            tasks.append(functools.partial(partial_own, c, j))
        return tasks

    def side_half(c):
        return [functools.partial(sideways, c, j) for j in range(1, places)]

    def side_part(c, piece_of):
        for j in range(1, places):
            sideways(c, j, piece_of, 2)

    def last_half(c):
        lo, n = chunks[c]
        return [functools.partial(homeward, c, k) for k in reversed(range(lo, lo + n))]

    def run(tasks, number):
        for _ in range(min(number, len(tasks))):
            tasks.pop(0)()

    waiting = []

    def events(c, tasks, lag):
        lo, n = chunks[c]
        steps = [(t, k) for k in range(lo, lo + n) for t in range(2)]
        for i, step in enumerate(steps):
            with jax.named_scope("relay%d_t%d_k%d" % (c, step[0], step[1])):
                relay(*step)
            waiting.append(step)
            if len(waiting) > lag:
                with jax.named_scope("pass%d" % c):
                    pass_on(*waiting.pop(0))
            if tasks:
                with jax.named_scope("work%d_%d" % (c, i)):
                    run(tasks, -(-len(tasks) // (len(steps) - i)))

    def settle(c):
        with jax.named_scope("settle%d" % c):
            while waiting and waiting[0][1] < chunks[c][0] + chunks[c][1]:
                pass_on(*waiting.pop(0))
            finish(c)

    never = 2 * groups
    events(0, [], 4)
    events(1, [], never)
    settle(0)
    events(2, first_half(0) + second_half(0), never)
    settle(1)
    with jax.named_scope("work1"):
        for task in first_half(1) + second_half(1) + side_half(1):
            task()
        side_part(0, 0)
    settle(2)
    with jax.named_scope("first2"):
        for task in first_half(2):
            task()
    for j in range(1, parts):
        remote(term, term_recv.at[own], term_send, term_sem.at[own],
               {"expert": lax.rem(own + j, parts)}).start()
    with jax.named_scope("second2"):
        for task in second_half(2) + side_half(2):
            task()
    with jax.named_scope("homeward1"):
        for task in last_half(1):
            task()
    side_part(0, 1)
    units = [functools.partial(grad_unit, m, r) for m in range(3) for r in range(parts)]
    with jax.named_scope("grads"):
        run(units, 1)
    with jax.named_scope("termwait"):
        for j in range(1, parts):
            arrived(term_recv.at[lax.rem(own + j, parts)], term_sem.at[lax.rem(own + j, parts)])
    term_recv[own] = term[...]
    whole = term_recv[0]
    for j in range(1, parts):
        whole = whole + term_recv[j]
    for i in range(rows // LANES):
        total[i] = whole[:, i * LANES : (i + 1) * LANES]
    for k in range(1, groups):
        remote(total.at[k // per_tile], home_s.at[k], back_send, back_recv.at[k],
               {"dp": ahead(k)}).start()
    with jax.named_scope("grads"):
        run(units, 1)
    with jax.named_scope("homeward2"):
        for task in last_half(2):
            task()
    with jax.named_scope("grads"):
        run(units, 2)
    for task in last_half(0):
        with jax.named_scope("homeward0"):
            task()
        with jax.named_scope("grads"):
            run(units, 1)
    with jax.named_scope("grads"):
        run(units, len(units))
    with jax.named_scope("collect0"):
        collect(0)
    with jax.named_scope("collect1"):
        collect(1)

    with jax.named_scope("gates"):
        for k in range(1, groups):
            arrived(home_s.at[k], back_recv.at[k])
        line = jnp.concatenate(
            [
                merge_tile(i, lambda k: home_s[k] if k else total[0])[0:1, :]
                for i in range(rows // LANES)
            ],
            axis=1,
        )
        spread = jnp.where(own_block, jnp.broadcast_to(line, (groups, rows)), 0.0)
        high = spread.astype(bf)
        rest = spread - high.astype(f32)
        mid = rest.astype(bf)
        low = (rest - mid.astype(f32)).astype(bf)
        picked = pick[...]
        found = matmul(high, picked) + matmul(mid, picked) + matmul(low, picked)
        for j in range(top):
            gg_out[j : j + 1, :] = jnp.sum(
                jnp.where(ids_ref[j : j + 1, :] == expert, found, 0.0), axis=0, keepdims=True
            )
    with jax.named_scope("collect2"):
        collect(2)

    arrived(scale_recv.at[pl.ds(1, groups - 1)], scale_out)
    arrived(home.at[pl.ds(0, groups - 1)], home_send)
    arrived(home_s.at[pl.ds(1, groups - 1)], back_send)
    arrived(term_recv.at[pl.ds(0, parts - 1)], term_send)
    arrived(recv_t.at[pl.ds(0, places), pl.ds(0, near - 1)], dp_near)
    arrived(recv_t.at[0, pl.ds(0, groups - near)], dp_far)
    arrived(recv_u.at[0, pl.ds(0, groups - 1)], dp_up)
    for t in range(2):
        arrived(recvs[t].at[pl.ds(0, places)], pair_fwd.at[t])
    if places > 1:
        arrived(recv_t.at[pl.ds(0, places - 1), pl.ds(0, groups - near)], side_fwd.at[0])
        arrived(recv_u.at[pl.ds(0, places - 1)], side_fwd.at[1])
    for j in range(places):
        for c in range(len(chunks)):
            pair(c, j).wait_send()
        if j:
            arrived(side_send.at[j], side_send_sem.at[j])


def put_out(*refs):
    number = len(refs) // 2
    sources, targets, sems = refs[:number], refs[number : 2 * number], refs[2 * number]
    copies = [
        pltpu.make_async_copy(sources[i], targets[i], sems.at[i]) for i in range(number)
    ]
    for copy in copies:
        copy.start()
    for copy in copies:
        copy.wait()


def exchange(ids, gates, tokens, upstream, w_gate, w_up, w_down, groups, parts, cap):
    top, count = ids.shape
    hid, width = w_gate.shape
    part = upstream.shape[1]
    rows = groups * cap
    places = parts // 2
    near = groups // 2
    bf, f32 = jnp.bfloat16, jnp.float32
    dma = pltpu.SemaphoreType.DMA
    vmem = pl.BlockSpec(memory_space=pltpu.VMEM)
    hbm = pl.BlockSpec(memory_space=pl.ANY)
    shapes = [((count, part), bf), ((top, count), f32)] + [((hid, width), bf)] * 3
    results = pl.pallas_call(
        functools.partial(kernel, groups, parts),
        out_shape=tuple(OUT(shape, kind) for shape, kind in shapes),
        in_specs=[vmem] * 2 + [hbm] * 5,
        out_specs=(vmem,) * 5,
        scratch_shapes=[
            pltpu.VMEM((places, count, part), bf),
            pltpu.VMEM((count, part), bf),
            pltpu.VMEM((rows, count), bf),
            pltpu.VMEM((places, groups, cap, part), bf),
            pltpu.VMEM((groups, cap, part), bf),
            pltpu.VMEM((parts, groups, cap, part), bf),
            pltpu.VMEM((parts, groups, cap, part), bf),
            pltpu.VMEM((3, parts, hid, part), bf),
            pltpu.VMEM((3, hid, rows), f32),
            pltpu.VMEM((3, hid, rows), bf),
            pltpu.VMEM((2, rows, hid), bf),
            pltpu.VMEM((rows // LANES, 8, LANES), f32),
            pltpu.VMEM((groups, 8, LANES), f32),
            pltpu.VMEM((8, rows), f32),
            pltpu.VMEM((8, rows), f32),
            pltpu.VMEM((parts, 8, rows), f32),
            pltpu.VMEM((rows // LANES, 8, LANES), f32),
            pltpu.VMEM((groups, 8, LANES), f32),
            pltpu.VMEM((places, groups, cap, part), bf),
            pltpu.VMEM((places, groups, cap, part), bf),
            pltpu.VMEM((places, groups, cap, part), bf),
            pltpu.VMEM((places, groups, cap, part), bf),
            pltpu.VMEM((places, groups, cap, part), f32),
            pltpu.VMEM((groups, cap, part), bf),
            pltpu.VMEM((groups, cap, part), bf),
            pltpu.VMEM((count, part), f32),
            dma((places + 1,)), dma((3, parts)), dma((2, parts, groups)), dma((groups,)),
            dma, dma, dma, dma((2,)), dma((2,)),
            dma, dma((places, 3)), dma((places, 3)), dma((places,)), dma((places, groups)),
            dma, dma((groups,)), dma, dma((parts,)), dma, dma((groups,)),
        ],
        compiler_params=pltpu.CompilerParams(
            collective_id=0, has_side_effects=True, vmem_limit_bytes=50 * 1024 * 1024
        ),
    )(ids, gates, tokens, upstream, w_gate, w_up, w_down)
    return pl.pallas_call(
        put_out,
        out_shape=tuple(jax.ShapeDtypeStruct(shape, kind) for shape, kind in shapes),
        in_specs=[vmem] * 5,
        out_specs=(hbm,) * 5,
        scratch_shapes=[dma((5,))],
        compiler_params=pltpu.CompilerParams(vmem_limit_bytes=2 * 1024 * 1024),
    )(*results)


def OUT(shape, kind):
    return pltpu.VMEM(shape, kind)


def per_device(tokens, upstream, gates, expert_ids, w_gate, w_up, w_down):
    groups = lax.axis_size("dp")
    parts = lax.axis_size("expert")
    experts = groups * w_gate.shape[0]
    cap = 2 * tokens.shape[0] * expert_ids.shape[1] // experts
    grad_x, grad_gates, grad_gate, grad_up, grad_down = exchange(
        expert_ids.T, gates.T, tokens, upstream, w_gate[0], w_up[0], w_down[0],
        groups, parts, cap,
    )
    return (grad_x, grad_gates.T, grad_gate[None], grad_up[None], grad_down[None])


def solution(mesh):
    in_specs = (
        P("dp", None),
        P("dp", "expert"),
        P("dp", None),
        P("dp", None),
        P("dp", "expert", None),
        P("dp", "expert", None),
        P("dp", "expert", None),
    )
    out_specs = (
        P("dp", "expert"),
        P("dp", None),
        P("dp", "expert", None),
        P("dp", "expert", None),
        P("dp", "expert", None),
    )
    return jax.shard_map(
        per_device, mesh=mesh, in_specs=in_specs, out_specs=out_specs, check_vma=False
    )
```
